32 devices in a mesh: mem: 8 (over z, core), tile: 4 (over y, x).
Axes of the slice: x: 2, y: 2, z: 4, core: 2. Of those that a mesh axis runs over, the one named last changes fastest.
Arguments:
- right_side: float32 [8, 32, 512], P(None, 'tile'), may hold values from -6 to 6
- members: bfloat16 [8, 8, 32, 512], P('mem', None, 'tile'), may hold values from -6 to 6
- diffusivity: float32 [8, 32, 512], P(None, 'tile'), may hold values from 0.02 to 0.12
- obs_index: int32 [8192], P('tile'), may hold values from 0 to 32767, as said below
- obs_precision: float32 [8192], P('tile'), may hold values from 0.5 to 4
Outputs:
- increment: float32 [8, 32, 512], P(None, 'tile')
- residual: float32 [8, 32, 512], P(None, 'tile')
The draws below stay inside these ranges and needn't reach their ends.
Inputs may be any that keep to these rules, and one draw needn't show every extreme that they name: `obs_index`: each entry is a flat cell index (level, row within the tile, column; column fastest) inside the block of the tile that holds the observation; several observations may share a cell.
All inputs are finite; a program needn't handle non-finite values.
Results may differ from the reference program's by a relative error of at most 0.0003.
Values sent between devices are 32-bit elements; how exact they have to be, the bound alone decides.
A program may use at most 64 MiB of HBM per device.

```python
import math
import jax
import jax.numpy as jnp
from jax import lax

NZ = 8
NX = 512
ROWS_DEV = 8
OBS_TILE = 2048
SWEEPS = 8
ITERS = 2
NY = 32
MEMBERS = 8
NOBS = 8192


def draw_obs_index(key, part):
    cells = NZ * ROWS_DEV * NX
    tiles = NOBS // OBS_TILE
    base = jax.random.randint(key, (tiles, OBS_TILE), 0, cells, dtype=jnp.int32)
    columns = jnp.arange(OBS_TILE, dtype=jnp.int32)[None, :]
    high_pos = jax.random.randint(jax.random.fold_in(key, 11), (tiles, 1), 0, OBS_TILE, dtype=jnp.int32)
    low_pos = (high_pos + 1) % OBS_TILE
    base = jnp.where(columns == high_pos, cells - 1, jnp.where(columns == low_pos, 0, base))
    return base.reshape(-1)


def level_of(own_key, dims, shards, smallest, high):
    factor_of = 1.0
    for axis_at, blocks in shards:
        heights = jax.random.uniform(jax.random.fold_in(jax.random.fold_in(own_key, 6), axis_at), (blocks,), jnp.float32, smallest / len(shards), high / len(shards))
        factor_of = factor_of * jnp.repeat(jnp.exp(heights), dims[axis_at] // blocks).reshape((-1,) + (1,) * (len(dims) - 1 - axis_at))
    return factor_of


def scatter_about(rng, dims, spread, limit, pieces=(), held_as=jnp.bfloat16):
    values = jax.random.normal(rng, dims, jnp.float32) * spread
    if len(pieces) > 0:
        values = level_of(rng, dims, pieces, -0.22, 0.18) * values
    return jnp.clip(values, min=-limit, max=limit).astype(held_as)


def setup_inputs(seed: int = 0) -> dict:
    arg_keys = jax.random.split(jax.random.key(seed), 6)
    right_side = scatter_about(arg_keys[0], (NZ, NY, NX), 1.0, 6.0, ((1, 4),), jnp.float32)
    members = scatter_about(arg_keys[1], (MEMBERS, NZ, NY, NX), 1.0, 6.0, ((0, 8), (2, 4)))
    diffusivity = jnp.clip(jnp.exp(math.log(0.12) - 1.7917595 * jax.random.uniform(arg_keys[2], (NZ, NY, NX), jnp.float32) ** level_of(arg_keys[2], (NZ, NY, NX), ((1, 4),), -0.2, 0.2)), 0.02, 0.12)
    obs_index = draw_obs_index(jax.random.fold_in(arg_keys[5], 71), 0)
    obs_precision = jnp.clip(jnp.exp(math.log(4.0) - 2.0794415 * jax.random.uniform(arg_keys[4], (NOBS,), jnp.float32) ** level_of(arg_keys[4], (NOBS,), ((0, 4),), -0.2, 0.2)), 0.5, 4.0)
    return dict(right_side=right_side, members=members, diffusivity=diffusivity, obs_index=obs_index, obs_precision=obs_precision)


def sweep(field, kappa):
    centre = field[:, 1:-1]
    middle = kappa[:, 1:-1]
    flux = 0.5 * (middle + kappa[:, 2:]) * (field[:, 2:] - centre)
    flux = flux + 0.5 * (middle + kappa[:, :-2]) * (field[:, :-2] - centre)
    fpad = jnp.pad(centre, ((0, 0), (0, 0), (1, 1)))
    kpad = jnp.pad(middle, ((0, 0), (0, 0), (1, 1)))
    flux = flux + 0.5 * (middle + kpad[:, :, 2:]) * (fpad[:, :, 2:] - centre)
    flux = flux + 0.5 * (middle + kpad[:, :, :-2]) * (fpad[:, :, :-2] - centre)
    return centre + flux


def reference(right_side, members, diffusivity, obs_index, obs_precision):
    tiles = jnp.arange(obs_index.shape[0], dtype=jnp.int32) // OBS_TILE
    level = obs_index // (ROWS_DEV * NX)
    row_pos = (obs_index // NX) % ROWS_DEV + tiles * ROWS_DEV
    column = obs_index % NX
    weight = jnp.zeros(right_side.shape, jnp.float32).at[level, row_pos, column].add(obs_precision)
    kappa_rim = jnp.pad(diffusivity, ((0, 0), (1, 1), (0, 0)))

    def localize(field):
        for step in range(SWEEPS):
            field = sweep(jnp.pad(field, ((0, 0), (1, 1), (0, 0))), kappa_rim)
        return field

    def operate(direction):
        def one_member(total, member):
            pert = member.astype(jnp.float32)
            return total + pert * localize(pert * direction), None

        total, unused = lax.scan(one_member, jnp.zeros(right_side.shape, jnp.float32), members)
        return direction + weight * direction + total / MEMBERS

    increment = jnp.zeros_like(right_side)
    residual, direction = right_side, right_side
    norm_now = jnp.sum(residual * residual)
    for step in range(ITERS):
        image = operate(direction)
        alpha = norm_now / jnp.sum(direction * image)
        increment = increment + alpha * direction
        residual = residual - alpha * image
        if step + 1 < ITERS:
            norm_next = jnp.sum(residual * residual)
            direction = residual + (norm_next / norm_now) * direction
            norm_now = norm_next
    return increment, residual
```

```python
import functools

import jax
import jax.numpy as jnp
from jax import lax
from jax.experimental import pallas as pl
from jax.experimental.pallas import tpu as pltpu
from jax.sharding import PartitionSpec as P

SWEEPS = 8
ITERS = 2
MESH = pl.DeviceIdType.MESH


def lanes_sum(x):
    total = x[:, 0:128]
    for j in range(1, x.shape[1] // 128):
        total = total + x[:, j * 128 : (j + 1) * 128]
    return jnp.sum(total, axis=0, keepdims=True)


def kernel(M, T, r0_ref, pert_ref, kap_ref, idx_ref, prec_ref, inc_ref, res_ref,
           pf, gat, halo_k, halo_r, halo_q, xt, cb, fld, tot, ext, q0a, q1a, st, sm,
           a_s, a_r, f_s, f_r, h_s, h_r, q_s, q_r, g_s, g_r, t_s, t_r, m_s, m_r):
    m = lax.axis_index("mem")
    t = lax.axis_index("tile")
    has_up = t > 0
    has_dn = t < T - 1
    levels, R, W = r0_ref.shape
    E = 3 * R
    sends = []

    def rc(src, dst, ss, rs, **dev):
        return pltpu.make_async_remote_copy(
            src_ref=src, dst_ref=dst, send_sem=ss, recv_sem=rs, device_id=dev, device_id_type=MESH)

    def rows_of(j):
        return pl.ds(pl.multiple_of(j * R, R), R)

    def mem_at(k):
        return lax.rem(m + k, M)

    def mem_from(k):
        return lax.rem(m + M - k, M)

    barrier = pltpu.get_barrier_semaphore()
    for k in range(1, M):
        pl.semaphore_signal(barrier, inc=1, device_id={"mem": mem_at(k)}, device_id_type=MESH)
    for k in range(1, T):
        pl.semaphore_signal(barrier, inc=1, device_id={"tile": lax.rem(t + k, T)}, device_id_type=MESH)
    pf[...] = pert_ref[0].astype(jnp.float32)
    pl.semaphore_wait(barrier, M + T - 2)

    def a2a(k):
        return rc(pf.at[mem_at(k)], gat.at[1, rows_of(m)], a_s.at[k], a_r.at[k], mem=mem_at(k))

    def a2a_in(k):
        return rc(pf.at[mem_at(k)], gat.at[1, rows_of(mem_from(k))], a_s.at[k], a_r.at[k], mem=mem_at(k))

    def pair(src, buf, s_sem, r_sem, base):
        up = rc(src, buf.at[1], s_sem.at[base], r_sem.at[base], tile=t - 1)
        dn = rc(src, buf.at[0], s_sem.at[base + 1], r_sem.at[base + 1], tile=t + 1)
        return up, dn

    def start_pair(p):
        @pl.when(has_up)
        def _():
            p[0].start()

        @pl.when(has_dn)
        def _():
            p[1].start()

    def recv_pair(p):
        @pl.when(has_dn)
        def _():
            p[0].wait_recv()

        @pl.when(has_up)
        def _():
            p[1].wait_recv()

    def send_pair(p):
        @pl.when(has_up)
        def _():
            p[0].wait_send()

        @pl.when(has_dn)
        def _():
            p[1].wait_send()

    def fwd(k):
        j = mem_from(k)
        src = pf.at[m] if k == 0 else gat.at[1, rows_of(j)]
        up = rc(src, gat.at[2, rows_of(j)], f_s.at[k], f_r.at[k], tile=t - 1)
        dn = rc(src, gat.at[0, rows_of(j)], f_s.at[M + k], f_r.at[M + k], tile=t + 1)
        return up, dn

    for k in range(1, M):
        a2a(k).start()
    start_pair(fwd(0))
    kp = pair(kap_ref.at[m], halo_k, h_s, h_r, 0)
    rp = pair(r0_ref.at[m], halo_r, h_s, h_r, 2)
    start_pair(kp)
    start_pair(rp)
    gat[1, rows_of(m), :] = pf[m]

    @pl.when(jnp.logical_not(has_up))
    def _():
        gat[0] = jnp.zeros_like(gat[0])
        halo_k[0] = jnp.zeros_like(halo_k[0])
        halo_r[0] = jnp.zeros_like(halo_r[0])
        halo_q[0] = jnp.zeros_like(halo_q[0])

    @pl.when(jnp.logical_not(has_dn))
    def _():
        gat[2] = jnp.zeros_like(gat[2])
        halo_k[1] = jnp.zeros_like(halo_k[1])
        halo_r[1] = jnp.zeros_like(halo_r[1])
        halo_q[1] = jnp.zeros_like(halo_q[1])

    nobs = idx_ref.shape[1]
    step_obs = 256 if nobs % 256 == 0 else nobs
    weight = jnp.zeros((R, W), jnp.float32)
    for c in range(nobs // step_obs):
        idx = idx_ref[:, c * step_obs : (c + 1) * step_obs]
        prec = prec_ref[:, c * step_obs : (c + 1) * step_obs]
        line = idx // W - m * R
        col = idx % W
        hit = lax.broadcasted_iota(jnp.int32, (R, step_obs), 0) == line
        left = jnp.where(hit, prec, 0.0)
        first = left.astype(jnp.bfloat16)
        rest = left - first.astype(jnp.float32)
        second = rest.astype(jnp.bfloat16)
        third = (rest - second.astype(jnp.float32)).astype(jnp.bfloat16)
        hot = (lax.broadcasted_iota(jnp.int32, (W, step_obs), 0) == col)
        hot = jnp.where(hot, 1.0, 0.0).astype(jnp.bfloat16)
        for piece in (first, second, third):
            weight = weight + lax.dot_general(
                piece, hot, (((1,), (1,)), ((), ())), preferred_element_type=jnp.float32)

    for k in range(1, M):
        a2a_in(k).wait_recv()
        start_pair(fwd(k))

    recv_pair(kp)
    recv_pair(rp)
    kx = jnp.concatenate([halo_k[0], kap_ref[m], halo_k[1]], axis=0)
    lane = lax.broadcasted_iota(jnp.int32, (E, W), 1)
    line = lax.broadcasted_iota(jnp.int32, (E, W), 0)
    inside = (line + (t - 1) * R >= 0) & (line + (t - 1) * R < T * R)
    east = jnp.where(lane == W - 1, 0.0, pltpu.roll(kx, W - 1, axis=1))
    west = jnp.where(lane == 0, 0.0, pltpu.roll(kx, 1, axis=1))
    north = pltpu.roll(kx, 1, axis=0)
    south = pltpu.roll(kx, E - 1, axis=0)
    ce = 0.5 * (kx + east)
    cw = 0.5 * (kx + west)
    cn = 0.5 * (kx + north)
    cs = 0.5 * (kx + south)
    ca = 1.0 - ((ce + cw) + (cn + cs))
    ce = jnp.where(lane == W - 1, 0.0, ce)
    cw = jnp.where(lane == 0, 0.0, cw)
    for i, c in enumerate((ca, ce, cw, cn, cs)):
        c = jnp.where(inside, c, 0.0)
        for e in range(1, E - 1):
            cb[i, e] = jnp.broadcast_to(c[e : e + 1], (M, W))

    for k in range(M):
        recv_pair(fwd(k))

    def localize(first):
        if first:
            for part in range(3):
                for j in range(W // 128):
                    cols = slice(j * 128, (j + 1) * 128)
                    block = gat[part, :, cols].reshape(M, R, 128)
                    xt[part * R : (part + 1) * R, :, cols] = jnp.swapaxes(block, 0, 1)
        for e in range(E):
            xe = xt[e]
            fld[0, e] = xe * jnp.broadcast_to(ext[e : e + 1, :], (M, W))
        for s in range(SWEEPS):
            a, b = s % 2, (s + 1) % 2
            count = E - 2 - 2 * s

            def one(i, carry, a=a, b=b, s=s):
                for u in range(2):
                    e = s + 1 + 2 * i + u
                    v = fld[a, e]
                    out = cb[0, e] * v
                    out = out + cb[1, e] * pltpu.roll(v, W - 1, axis=1)
                    out = out + cb[2, e] * pltpu.roll(v, 1, axis=1)
                    out = out + cb[3, e] * fld[a, e - 1]
                    out = out + cb[4, e] * fld[a, e + 1]
                    fld[b, e] = out
                return carry

            lax.fori_loop(0, count // 2, one, 0)
        z = SWEEPS % 2
        for r in range(R):
            tot[r : r + 1, :] = jnp.sum(xt[R + r] * fld[z, R + r], axis=0, keepdims=True)
        return tot[...]

    def gather(buf, base):
        out = []
        for k in range(1, M):
            out.append(rc(buf.at[m], buf.at[m], g_s.at[base + k], g_r.at[base + k], mem=mem_at(k)))
        return out

    def gather_in(buf, base):
        for k in range(1, M):
            j = mem_from(k)
            rc(buf.at[j], buf.at[j], g_s.at[base + k], g_r.at[base + k], mem=mem_at(k)).wait_recv()

    def tile_sum_start(n, vals):
        zero = jnp.zeros((8 - len(vals), 128), jnp.float32)
        st[n, t] = jnp.concatenate(list(vals) + [zero], axis=0)
        for k in range(1, T):
            c = rc(st.at[n, t], st.at[n, t], t_s.at[n * T + k], t_r.at[n * T + k], tile=lax.rem(t + k, T))
            c.start()
            sends.append(c)

    def mem_sum_start(n):
        for k in range(1, T):
            j = lax.rem(t + T - k, T)
            rc(st.at[n, j], st.at[n, j], t_s.at[n * T + k], t_r.at[n * T + k], tile=lax.rem(t + k, T)).wait_recv()
        total = st[n, 0]
        for j in range(1, T):
            total = total + st[n, j]
        sm[n, m] = total
        for k in range(1, M):
            c = rc(sm.at[n, m], sm.at[n, m], m_s.at[n * M + k], m_r.at[n * M + k], mem=mem_at(k))
            c.start()
            sends.append(c)

    def mem_sum_end(n):
        for k in range(1, M):
            j = mem_from(k)
            rc(sm.at[n, j], sm.at[n, j], m_s.at[n * M + k], m_r.at[n * M + k], mem=mem_at(k)).wait_recv()
        total = sm[n, 0]
        for j in range(1, M):
            total = total + sm[n, j]
        return jnp.sum(total, axis=1, keepdims=True)

    inv = 1.0 / M
    r0 = r0_ref[m]
    ext[0:R] = halo_r[0]
    ext[R : 2 * R] = r0
    ext[2 * R : E] = halo_r[1]
    q0 = r0 + weight * r0 + localize(True) * inv
    q0a[m] = q0
    qp = pair(q0a.at[m], halo_q, q_s, q_r, 0)
    start_pair(qp)
    tile_sum_start(0, (lanes_sum(r0 * r0), lanes_sum(r0 * q0)))
    g0 = gather(q0a, 0)
    for c in g0:
        c.start()
    recv_pair(qp)
    mem_sum_start(0)
    ext[0:R] = halo_q[0]
    ext[R : 2 * R] = q0
    ext[2 * R : E] = halo_q[1]
    q1 = q0 + weight * q0 + localize(False) * inv
    q1a[m] = q1
    g1 = gather(q1a, M)
    for c in g1:
        c.start()
    dots = mem_sum_end(0)
    rr, rq = dots[0:1], dots[1:2]
    alpha = rr / rq
    r1 = r0 - alpha * q0
    ar1 = q0 - alpha * q1
    tile_sum_start(1, (lanes_sum(r1 * r1), lanes_sum(r1 * ar1), lanes_sum(r1 * q0)))
    mem_sum_start(1)
    gather_in(q0a, 0)
    gather_in(q1a, M)
    dots = mem_sum_end(1)
    new = dots[0:1]
    beta = new / rr
    den = dots[1:2] + 2.0 * beta * dots[2:3] + beta * beta * rq
    alpha2 = new / den
    for l in range(levels):
        b = r0_ref[l]
        q = q0a[l]
        r1 = b - alpha * q
        inc_ref[l] = alpha * b + alpha2 * (r1 + beta * b)
        res_ref[l] = r1 - alpha2 * ((q - alpha * q1a[l]) + beta * q)

    for k in range(1, M):
        a2a(k).wait_send()
    for k in range(M):
        send_pair(fwd(k))
    send_pair(kp)
    send_pair(rp)
    send_pair(qp)
    for c in g0 + g1 + sends:
        c.wait_send()


def fused(M, T, right_side, members, diffusivity, obs_index, obs_precision):
    levels, R, W = right_side.shape
    f32 = jnp.float32
    dma = pltpu.SemaphoreType.DMA
    vmem = pl.BlockSpec(memory_space=pltpu.VMEM)
    out = jax.ShapeDtypeStruct(right_side.shape, f32)
    E = 3 * R
    return pl.pallas_call(
        functools.partial(kernel, M, T),
        name="cg",
        out_shape=(out, out),
        in_specs=[vmem] * 5,
        out_specs=(vmem, vmem),
        scratch_shapes=[
            pltpu.VMEM((levels, R, W), f32),
            pltpu.VMEM((3, M * R, W), f32),
            pltpu.VMEM((2, R, W), f32),
            pltpu.VMEM((2, R, W), f32),
            pltpu.VMEM((2, R, W), f32),
            pltpu.VMEM((E, M, W), f32),
            pltpu.VMEM((5, E, M, W), f32),
            pltpu.VMEM((2, E, M, W), f32),
            pltpu.VMEM((R, W), f32),
            pltpu.VMEM((E, W), f32),
            pltpu.VMEM((levels, R, W), f32),
            pltpu.VMEM((levels, R, W), f32),
            pltpu.VMEM((2, T, 8, 128), f32),
            pltpu.VMEM((2, M, 8, 128), f32),
            dma((M,)), dma((M,)),
            dma((2 * M,)), dma((2 * M,)),
            dma((4,)), dma((4,)),
            dma((2,)), dma((2,)),
            dma((2 * M,)), dma((2 * M,)),
            dma((2 * T,)), dma((2 * T,)),
            dma((2 * M,)), dma((2 * M,)),
        ],
        compiler_params=pltpu.CompilerParams(
            collective_id=0, has_side_effects=True, vmem_limit_bytes=40 * 1024 * 1024),
    )(right_side, members, diffusivity, obs_index.reshape(1, -1), obs_precision.reshape(1, -1))


def padded(shard, sides, width):
    for axis, dim in sides:
        size, length = (lax.axis_size(axis), shard.shape[dim])
        up = [(i, (i + 1) % size) for i in range(size - 1)]
        down = [(j, i) for i, j in up]
        last = lax.slice_in_dim(shard, length - width, length, axis=dim)
        leading = lax.slice_in_dim(shard, 0, width, axis=dim)
        before = lax.ppermute(last, axis, up)
        after = lax.ppermute(leading, axis, down)
        shard = jnp.concatenate([before, shard, after], axis=dim)
    return shard


def sweep(field, kappa):
    centre = field[:, 1:-1]
    middle = kappa[:, 1:-1]
    flux = 0.5 * (middle + kappa[:, 2:]) * (field[:, 2:] - centre)
    flux = flux + 0.5 * (middle + kappa[:, :-2]) * (field[:, :-2] - centre)
    fpad = jnp.pad(centre, ((0, 0), (0, 0), (1, 1)))
    kpad = jnp.pad(middle, ((0, 0), (0, 0), (1, 1)))
    flux = flux + 0.5 * (middle + kpad[:, :, 2:]) * (fpad[:, :, 2:] - centre)
    flux = flux + 0.5 * (middle + kpad[:, :, :-2]) * (fpad[:, :, :-2] - centre)
    return centre + flux


def general(right_side, members, diffusivity, obs_index, obs_precision):
    levels, rows, width = right_side.shape
    level = obs_index // (rows * width)
    row_pos = obs_index // width % rows
    column = obs_index % width
    weight = jnp.zeros(right_side.shape, jnp.float32).at[level, row_pos, column].add(obs_precision)
    tile_pos = lax.axis_index("tile")
    all_rows = rows * lax.axis_size("tile")
    total_members = members.shape[0] * lax.axis_size("mem")
    depth_rim = SWEEPS
    kappa_rim = padded(diffusivity, (("tile", 1),), depth_rim)

    def inner(first, second):
        return lax.psum(jnp.sum(first * second), "tile")

    increment = jnp.zeros_like(right_side)
    residual, direction = (right_side, right_side)
    norm_now = inner(residual, residual)
    for step in range(ITERS):
        pert = members[0].astype(jnp.float32)
        extended = padded(pert * direction, (("tile", 1),), SWEEPS)
        for localize_step in range(SWEEPS):
            depth = SWEEPS - localize_step - 1
            kappa = kappa_rim[:, localize_step : kappa_rim.shape[1] - localize_step]
            extended = sweep(extended, kappa)
            global_row = tile_pos * rows - depth + jnp.arange(rows + 2 * depth, dtype=jnp.int32)
            inside = (global_row >= 0) & (global_row < all_rows)
            extended = jnp.where(inside[None, :, None], extended, 0.0)
        total = pert * extended
        operate_total = lax.psum(total, "mem")
        image = direction + weight * direction + operate_total / total_members
        alpha = norm_now / inner(direction, image)
        increment = increment + alpha * direction
        residual = residual - alpha * image
        if step + 1 < ITERS:
            norm_next = inner(residual, residual)
            direction = residual + norm_next / norm_now * direction
            norm_now = norm_next
    return (increment, residual)


def solution(mesh):
    in_specs = (
        P(None, "tile", None),
        P("mem", None, "tile", None),
        P(None, "tile", None),
        P("tile"),
        P("tile"),
    )
    out_specs = (P(None, "tile", None), P(None, "tile", None))
    M, T = mesh.shape["mem"], mesh.shape["tile"]

    def local(right_side, members, diffusivity, obs_index, obs_precision):
        levels, rows, width = right_side.shape
        fits = levels == M and members.shape[0] == 1 and rows == SWEEPS and M == 8
        if fits and ITERS == 2 and width % 128 == 0:
            return fused(M, T, right_side, members, diffusivity, obs_index, obs_precision)
        return general(right_side, members, diffusivity, obs_index, obs_precision)

    return jax.shard_map(local, mesh=mesh, in_specs=in_specs, out_specs=out_specs, check_vma=False)
```

```python
import functools

import jax
import jax.numpy as jnp
from jax import lax
from jax.experimental import pallas as pl
from jax.experimental.pallas import tpu as pltpu
from jax.sharding import PartitionSpec as P

SWEEPS = 8
ITERS = 2
MESH = pl.DeviceIdType.MESH


def lanes_sum(x):
    total = x[:, 0:128]
    for j in range(1, x.shape[1] // 128):
        total = total + x[:, j * 128 : (j + 1) * 128]
    return jnp.sum(total, axis=0, keepdims=True)


def kernel(M, T, r0_hbm, pert_hbm, kap_hbm, idx_hbm, prec_hbm, inc_ref, res_ref,
           r0_ref, pert_ref, kap_ref, idx_ref, prec_ref, l_s, pf, gat, halo_k, halo_r, halo_q, xt, cb, fld, tot, ext, q0a, q1a, st, sm,
           a_s, a_r, f_s, f_r, h_s, h_r, q_s, q_r, g_s, g_r, t_s, t_r, m_s, m_r):
    m = lax.axis_index("mem")
    t = lax.axis_index("tile")
    has_up = t > 0
    has_dn = t < T - 1
    levels, R, W = r0_ref.shape
    E = 3 * R
    sends = []

    def rc(src, dst, ss, rs, **dev):
        return pltpu.make_async_remote_copy(
            src_ref=src, dst_ref=dst, send_sem=ss, recv_sem=rs, device_id=dev, device_id_type=MESH)

    def rows_of(j):
        return pl.ds(pl.multiple_of(j * R, R), R)

    def mem_at(k):
        return lax.rem(m + k, M)

    def mem_from(k):
        return lax.rem(m + M - k, M)

    loads = [
        pltpu.make_async_copy(pert_hbm.at[0], pert_ref, l_s.at[0]),
        pltpu.make_async_copy(kap_hbm.at[m], kap_ref, l_s.at[1]),
        pltpu.make_async_copy(r0_hbm, r0_ref, l_s.at[2]),
        pltpu.make_async_copy(idx_hbm, idx_ref, l_s.at[3]),
        pltpu.make_async_copy(prec_hbm, prec_ref, l_s.at[4]),
    ]
    for c in loads:
        c.start()

    barrier = pltpu.get_barrier_semaphore()
    for k in range(1, M):
        pl.semaphore_signal(barrier, inc=1, device_id={"mem": mem_at(k)}, device_id_type=MESH)
    for k in range(1, T):
        pl.semaphore_signal(barrier, inc=1, device_id={"tile": lax.rem(t + k, T)}, device_id_type=MESH)
    loads[0].wait()
    pf[...] = pert_ref[...].astype(jnp.float32)
    pl.semaphore_wait(barrier, M + T - 2)

    def a2a(k):
        return rc(pf.at[mem_at(k)], gat.at[1, rows_of(m)], a_s.at[k], a_r.at[k], mem=mem_at(k))

    def a2a_in(k):
        return rc(pf.at[mem_at(k)], gat.at[1, rows_of(mem_from(k))], a_s.at[k], a_r.at[k], mem=mem_at(k))

    def pair(src, buf, s_sem, r_sem, base):
        up = rc(src, buf.at[1], s_sem.at[base], r_sem.at[base], tile=t - 1)
        dn = rc(src, buf.at[0], s_sem.at[base + 1], r_sem.at[base + 1], tile=t + 1)
        return up, dn

    def start_pair(p):
        @pl.when(has_up)
        def _():
            p[0].start()

        @pl.when(has_dn)
        def _():
            p[1].start()

    def recv_pair(p):
        @pl.when(has_dn)
        def _():
            p[0].wait_recv()

        @pl.when(has_up)
        def _():
            p[1].wait_recv()

    def send_pair(p):
        @pl.when(has_up)
        def _():
            p[0].wait_send()

        @pl.when(has_dn)
        def _():
            p[1].wait_send()

    def fwd(k):
        j = mem_from(k)
        src = pf.at[m] if k == 0 else gat.at[1, rows_of(j)]
        up = rc(src, gat.at[2, rows_of(j)], f_s.at[k], f_r.at[k], tile=t - 1)
        dn = rc(src, gat.at[0, rows_of(j)], f_s.at[M + k], f_r.at[M + k], tile=t + 1)
        return up, dn

    for k in range(1, M):
        a2a(k).start()
    start_pair(fwd(0))
    loads[1].wait()
    loads[2].wait()
    kp = pair(kap_ref, halo_k, h_s, h_r, 0)
    rp = pair(r0_ref.at[m], halo_r, h_s, h_r, 2)
    start_pair(kp)
    start_pair(rp)
    gat[1, rows_of(m), :] = pf[m]

    @pl.when(jnp.logical_not(has_up))
    def _():
        gat[0] = jnp.zeros_like(gat[0])
        halo_k[0] = jnp.zeros_like(halo_k[0])
        halo_r[0] = jnp.zeros_like(halo_r[0])
        halo_q[0] = jnp.zeros_like(halo_q[0])

    @pl.when(jnp.logical_not(has_dn))
    def _():
        gat[2] = jnp.zeros_like(gat[2])
        halo_k[1] = jnp.zeros_like(halo_k[1])
        halo_r[1] = jnp.zeros_like(halo_r[1])
        halo_q[1] = jnp.zeros_like(halo_q[1])

    loads[3].wait()
    loads[4].wait()
    nobs = idx_ref.shape[1]
    step_obs = 256 if nobs % 256 == 0 else nobs
    weight = jnp.zeros((R, W), jnp.float32)
    for c in range(nobs // step_obs):
        idx = idx_ref[:, c * step_obs : (c + 1) * step_obs]
        prec = prec_ref[:, c * step_obs : (c + 1) * step_obs]
        line = idx // W - m * R
        col = idx % W
        hit = lax.broadcasted_iota(jnp.int32, (R, step_obs), 0) == line
        left = jnp.where(hit, prec, 0.0)
        first = left.astype(jnp.bfloat16)
        rest = left - first.astype(jnp.float32)
        second = rest.astype(jnp.bfloat16)
        third = (rest - second.astype(jnp.float32)).astype(jnp.bfloat16)
        hot = (lax.broadcasted_iota(jnp.int32, (W, step_obs), 0) == col)
        hot = jnp.where(hot, 1.0, 0.0).astype(jnp.bfloat16)
        for piece in (first, second, third):
            weight = weight + lax.dot_general(
                piece, hot, (((1,), (1,)), ((), ())), preferred_element_type=jnp.float32)

    for k in range(1, M):
        a2a_in(k).wait_recv()
        start_pair(fwd(k))

    recv_pair(kp)
    recv_pair(rp)
    kx = jnp.concatenate([halo_k[0], kap_ref[...], halo_k[1]], axis=0)
    lane = lax.broadcasted_iota(jnp.int32, (E, W), 1)
    line = lax.broadcasted_iota(jnp.int32, (E, W), 0)
    inside = (line + (t - 1) * R >= 0) & (line + (t - 1) * R < T * R)
    east = jnp.where(lane == W - 1, 0.0, pltpu.roll(kx, W - 1, axis=1))
    west = jnp.where(lane == 0, 0.0, pltpu.roll(kx, 1, axis=1))
    north = pltpu.roll(kx, 1, axis=0)
    south = pltpu.roll(kx, E - 1, axis=0)
    ce = 0.5 * (kx + east)
    cw = 0.5 * (kx + west)
    cn = 0.5 * (kx + north)
    cs = 0.5 * (kx + south)
    ca = 1.0 - ((ce + cw) + (cn + cs))
    ce = jnp.where(lane == W - 1, 0.0, ce)
    cw = jnp.where(lane == 0, 0.0, cw)
    for i, c in enumerate((ca, ce, cw, cn, cs)):
        c = jnp.where(inside, c, 0.0)
        for e in range(1, E - 1):
            cb[i, e] = jnp.broadcast_to(c[e : e + 1], (M, W))

    def turn(part):
        for j in range(W // 128):
            cols = slice(j * 128, (j + 1) * 128)
            block = gat[part, :, cols].reshape(M, R, 128)
            xt[part * R : (part + 1) * R, :, cols] = jnp.swapaxes(block, 0, 1)

    turn(1)
    for k in range(M):
        recv_pair(fwd(k))
    turn(0)
    turn(2)

    def localize():
        for e in range(E):
            xe = xt[e]
            fld[0, e] = xe * jnp.broadcast_to(ext[e : e + 1, :], (M, W))
        for s in range(SWEEPS):
            a, b = s % 2, (s + 1) % 2
            above, here = fld[a, s], fld[a, s + 1]
            for e in range(s + 1, E - 1 - s):
                below = fld[a, e + 1]
                out = cb[0, e] * here
                out = out + cb[3, e] * above
                out = out + cb[4, e] * below
                out = out + cb[1, e] * pltpu.roll(here, W - 1, axis=1)
                out = out + cb[2, e] * pltpu.roll(here, 1, axis=1)
                fld[b, e] = out
                above, here = here, below
        z = SWEEPS % 2
        for r in range(R):
            tot[r : r + 1, :] = jnp.sum(xt[R + r] * fld[z, R + r], axis=0, keepdims=True)
        return tot[...]

    def gather(buf, base):
        out = []
        for k in range(1, M):
            out.append(rc(buf.at[m], buf.at[m], g_s.at[base + k], g_r.at[base + k], mem=mem_at(k)))
        return out

    def gather_in(buf, base):
        for k in range(1, M):
            j = mem_from(k)
            rc(buf.at[j], buf.at[j], g_s.at[base + k], g_r.at[base + k], mem=mem_at(k)).wait_recv()

    def tile_sum_start(n, vals):
        zero = jnp.zeros((8 - len(vals), 128), jnp.float32)
        st[n, t] = jnp.concatenate(list(vals) + [zero], axis=0)
        for k in range(1, T):
            c = rc(st.at[n, t], st.at[n, t], t_s.at[n * T + k], t_r.at[n * T + k], tile=lax.rem(t + k, T))
            c.start()
            sends.append(c)

    def mem_sum_start(n):
        for k in range(1, T):
            j = lax.rem(t + T - k, T)
            rc(st.at[n, j], st.at[n, j], t_s.at[n * T + k], t_r.at[n * T + k], tile=lax.rem(t + k, T)).wait_recv()
        total = st[n, 0]
        for j in range(1, T):
            total = total + st[n, j]
        sm[n, m] = total
        for k in range(1, M):
            c = rc(sm.at[n, m], sm.at[n, m], m_s.at[n * M + k], m_r.at[n * M + k], mem=mem_at(k))
            c.start()
            sends.append(c)

    def mem_sum_end(n):
        for k in range(1, M):
            j = mem_from(k)
            rc(sm.at[n, j], sm.at[n, j], m_s.at[n * M + k], m_r.at[n * M + k], mem=mem_at(k)).wait_recv()
        total = sm[n, 0]
        for j in range(1, M):
            total = total + sm[n, j]
        return jnp.sum(total, axis=1, keepdims=True)

    inv = 1.0 / M
    r0 = r0_ref[m]
    ext[0:R] = halo_r[0]
    ext[R : 2 * R] = r0
    ext[2 * R : E] = halo_r[1]
    q0 = r0 + weight * r0 + localize() * inv
    q0a[m] = q0
    qp = pair(q0a.at[m], halo_q, q_s, q_r, 0)
    start_pair(qp)
    tile_sum_start(0, (lanes_sum(r0 * r0), lanes_sum(r0 * q0)))
    g0 = gather(q0a, 0)
    for c in g0:
        c.start()
    recv_pair(qp)
    mem_sum_start(0)
    ext[0:R] = halo_q[0]
    ext[R : 2 * R] = q0
    ext[2 * R : E] = halo_q[1]
    q1 = q0 + weight * q0 + localize() * inv
    q1a[m] = q1
    g1 = gather(q1a, M)
    for c in g1:
        c.start()
    dots = mem_sum_end(0)
    rr, rq = dots[0:1], dots[1:2]
    alpha = rr / rq
    r1 = r0 - alpha * q0
    ar1 = q0 - alpha * q1
    tile_sum_start(1, (lanes_sum(r1 * r1), lanes_sum(r1 * ar1), lanes_sum(r1 * q0)))
    mem_sum_start(1)
    gather_in(q0a, 0)
    gather_in(q1a, M)
    dots = mem_sum_end(1)
    new = dots[0:1]
    beta = new / rr
    den = dots[1:2] + 2.0 * beta * dots[2:3] + beta * beta * rq
    alpha2 = new / den
    for l in range(levels):
        b = r0_ref[l]
        q = q0a[l]
        r1 = b - alpha * q
        inc_ref[l] = alpha * b + alpha2 * (r1 + beta * b)
        res_ref[l] = r1 - alpha2 * ((q - alpha * q1a[l]) + beta * q)

    for k in range(1, M):
        a2a(k).wait_send()
    for k in range(M):
        send_pair(fwd(k))
    send_pair(kp)
    send_pair(rp)
    send_pair(qp)
    for c in g0 + g1 + sends:
        c.wait_send()


def fused(M, T, right_side, members, diffusivity, obs_index, obs_precision):
    levels, R, W = right_side.shape
    f32 = jnp.float32
    dma = pltpu.SemaphoreType.DMA
    vmem = pl.BlockSpec(memory_space=pltpu.VMEM)
    out = jax.ShapeDtypeStruct(right_side.shape, f32)
    E = 3 * R
    return pl.pallas_call(
        functools.partial(kernel, M, T),
        name="cg",
        out_shape=(out, out),
        in_specs=[pl.BlockSpec(memory_space=pltpu.HBM)] * 5,
        out_specs=(vmem, vmem),
        scratch_shapes=[
            pltpu.VMEM((levels, R, W), f32),
            pltpu.VMEM((levels, R, W), members.dtype),
            pltpu.VMEM((R, W), f32),
            pltpu.VMEM((1, obs_index.shape[0]), jnp.int32),
            pltpu.VMEM((1, obs_index.shape[0]), f32),
            dma((5,)),
            pltpu.VMEM((levels, R, W), f32),
            pltpu.VMEM((3, M * R, W), f32),
            pltpu.VMEM((2, R, W), f32),
            pltpu.VMEM((2, R, W), f32),
            pltpu.VMEM((2, R, W), f32),
            pltpu.VMEM((E, M, W), f32),
            pltpu.VMEM((5, E, M, W), f32),
            pltpu.VMEM((2, E, M, W), f32),
            pltpu.VMEM((R, W), f32),
            pltpu.VMEM((E, W), f32),
            pltpu.VMEM((levels, R, W), f32),
            pltpu.VMEM((levels, R, W), f32),
            pltpu.VMEM((2, T, 8, 128), f32),
            pltpu.VMEM((2, M, 8, 128), f32),
            dma((M,)), dma((M,)),
            dma((2 * M,)), dma((2 * M,)),
            dma((4,)), dma((4,)),
            dma((2,)), dma((2,)),
            dma((2 * M,)), dma((2 * M,)),
            dma((2 * T,)), dma((2 * T,)),
            dma((2 * M,)), dma((2 * M,)),
        ],
        compiler_params=pltpu.CompilerParams(
            collective_id=0, has_side_effects=True),
    )(right_side, members, diffusivity, obs_index.reshape(1, -1), obs_precision.reshape(1, -1))


def padded(shard, sides, width):
    for axis, dim in sides:
        size, length = (lax.axis_size(axis), shard.shape[dim])
        up = [(i, (i + 1) % size) for i in range(size - 1)]
        down = [(j, i) for i, j in up]
        last = lax.slice_in_dim(shard, length - width, length, axis=dim)
        leading = lax.slice_in_dim(shard, 0, width, axis=dim)
        before = lax.ppermute(last, axis, up)
        after = lax.ppermute(leading, axis, down)
        shard = jnp.concatenate([before, shard, after], axis=dim)
    return shard


def sweep(field, kappa):
    centre = field[:, 1:-1]
    middle = kappa[:, 1:-1]
    flux = 0.5 * (middle + kappa[:, 2:]) * (field[:, 2:] - centre)
    flux = flux + 0.5 * (middle + kappa[:, :-2]) * (field[:, :-2] - centre)
    fpad = jnp.pad(centre, ((0, 0), (0, 0), (1, 1)))
    kpad = jnp.pad(middle, ((0, 0), (0, 0), (1, 1)))
    flux = flux + 0.5 * (middle + kpad[:, :, 2:]) * (fpad[:, :, 2:] - centre)
    flux = flux + 0.5 * (middle + kpad[:, :, :-2]) * (fpad[:, :, :-2] - centre)
    return centre + flux


def general(right_side, members, diffusivity, obs_index, obs_precision):
    levels, rows, width = right_side.shape
    level = obs_index // (rows * width)
    row_pos = obs_index // width % rows
    column = obs_index % width
    weight = jnp.zeros(right_side.shape, jnp.float32).at[level, row_pos, column].add(obs_precision)
    tile_pos = lax.axis_index("tile")
    all_rows = rows * lax.axis_size("tile")
    total_members = members.shape[0] * lax.axis_size("mem")
    depth_rim = SWEEPS
    kappa_rim = padded(diffusivity, (("tile", 1),), depth_rim)

    def inner(first, second):
        return lax.psum(jnp.sum(first * second), "tile")

    increment = jnp.zeros_like(right_side)
    residual, direction = (right_side, right_side)
    norm_now = inner(residual, residual)
    for step in range(ITERS):
        pert = members[0].astype(jnp.float32)
        extended = padded(pert * direction, (("tile", 1),), SWEEPS)
        for localize_step in range(SWEEPS):
            depth = SWEEPS - localize_step - 1
            kappa = kappa_rim[:, localize_step : kappa_rim.shape[1] - localize_step]
            extended = sweep(extended, kappa)
            global_row = tile_pos * rows - depth + jnp.arange(rows + 2 * depth, dtype=jnp.int32)
            inside = (global_row >= 0) & (global_row < all_rows)
            extended = jnp.where(inside[None, :, None], extended, 0.0)
        total = pert * extended
        operate_total = lax.psum(total, "mem")
        image = direction + weight * direction + operate_total / total_members
        alpha = norm_now / inner(direction, image)
        increment = increment + alpha * direction
        residual = residual - alpha * image
        if step + 1 < ITERS:
            norm_next = inner(residual, residual)
            direction = residual + norm_next / norm_now * direction
            norm_now = norm_next
    return (increment, residual)


def solution(mesh):
    in_specs = (
        P(None, "tile", None),
        P("mem", None, "tile", None),
        P(None, "tile", None),
        P("tile"),
        P("tile"),
    )
    out_specs = (P(None, "tile", None), P(None, "tile", None))
    M, T = mesh.shape["mem"], mesh.shape["tile"]

    def local(right_side, members, diffusivity, obs_index, obs_precision):
        levels, rows, width = right_side.shape
        fits = levels == M and members.shape[0] == 1 and rows == SWEEPS and M == 8
        if fits and ITERS == 2 and width % 128 == 0:
            return fused(M, T, right_side, members, diffusivity, obs_index, obs_precision)
        return general(right_side, members, diffusivity, obs_index, obs_precision)

    return jax.shard_map(local, mesh=mesh, in_specs=in_specs, out_specs=out_specs, check_vma=False)
```

```python
import functools

import jax
import jax.numpy as jnp
from jax import lax
from jax.experimental import pallas as pl
from jax.experimental.pallas import tpu as pltpu
from jax.sharding import PartitionSpec as P

SWEEPS = 8
ITERS = 2
MESH = pl.DeviceIdType.MESH


def lanes_sum(x):
    total = x[:, 0:128]
    for j in range(1, x.shape[1] // 128):
        total = total + x[:, j * 128 : (j + 1) * 128]
    return jnp.sum(total, axis=0, keepdims=True)


def kernel(M, T, r0_hbm, pert_hbm, kap_hbm, idx_hbm, prec_hbm, inc_ref, res_ref,
           r0_ref, pert_ref, kap_ref, idx_ref, prec_ref, l_s, pf, gat, halo_k, halo_r, halo_q, xt, cb, fld, tot, ext, q0a, q1a, st, go,
           a_s, a_r, f_s, f_r, h_s, h_r, q_s, q_r, g_s, g_r, t_s, t_r):
    m = lax.axis_index("mem")
    t = lax.axis_index("tile")
    has_up = t > 0
    has_dn = t < T - 1
    levels, R, W = r0_ref.shape
    E = 3 * R
    sends = []

    def rc(src, dst, ss, rs, **dev):
        return pltpu.make_async_remote_copy(
            src_ref=src, dst_ref=dst, send_sem=ss, recv_sem=rs, device_id=dev, device_id_type=MESH)

    def rows_of(j):
        return pl.ds(pl.multiple_of(j * R, R), R)

    def mem_at(k):
        return lax.rem(m + k, M)

    def mem_from(k):
        return lax.rem(m + M - k, M)

    loads = [
        pltpu.make_async_copy(pert_hbm.at[0], pert_ref, l_s.at[0]),
        pltpu.make_async_copy(kap_hbm.at[m], kap_ref, l_s.at[1]),
        pltpu.make_async_copy(r0_hbm, r0_ref, l_s.at[2]),
        pltpu.make_async_copy(idx_hbm, idx_ref, l_s.at[3]),
        pltpu.make_async_copy(prec_hbm, prec_ref, l_s.at[4]),
    ]
    for c in loads:
        c.start()

    barrier = pltpu.get_barrier_semaphore()
    for k in range(1, M):
        pl.semaphore_signal(barrier, inc=1, device_id={"mem": mem_at(k)}, device_id_type=MESH)
    for k in range(1, T):
        pl.semaphore_signal(barrier, inc=1, device_id={"tile": lax.rem(t + k, T)}, device_id_type=MESH)
    loads[0].wait()
    pf[...] = pert_ref[...].astype(jnp.float32)
    pl.semaphore_wait(barrier, M + T - 2)
    for k in range(1, T):
        pl.semaphore_signal(go, inc=1, device_id={"tile": lax.rem(t + k, T)}, device_id_type=MESH)

    def a2a(k):
        return rc(pf.at[mem_at(k)], gat.at[1, rows_of(m)], a_s.at[k], a_r.at[k], mem=mem_at(k))

    def a2a_in(k):
        return rc(pf.at[mem_at(k)], gat.at[1, rows_of(mem_from(k))], a_s.at[k], a_r.at[k], mem=mem_at(k))

    def pair(src, buf, s_sem, r_sem, base):
        up = rc(src, buf.at[1], s_sem.at[base], r_sem.at[base], tile=t - 1)
        dn = rc(src, buf.at[0], s_sem.at[base + 1], r_sem.at[base + 1], tile=t + 1)
        return up, dn

    def start_pair(p):
        @pl.when(has_up)
        def _():
            p[0].start()

        @pl.when(has_dn)
        def _():
            p[1].start()

    def recv_pair(p):
        @pl.when(has_dn)
        def _():
            p[0].wait_recv()

        @pl.when(has_up)
        def _():
            p[1].wait_recv()

    def send_pair(p):
        @pl.when(has_up)
        def _():
            p[0].wait_send()

        @pl.when(has_dn)
        def _():
            p[1].wait_send()

    def fwd(k):
        j = mem_from(k)
        src = pf.at[m] if k == 0 else gat.at[1, rows_of(j)]
        up = rc(src, gat.at[2, rows_of(j)], f_s.at[k], f_r.at[k], tile=t - 1)
        dn = rc(src, gat.at[0, rows_of(j)], f_s.at[M + k], f_r.at[M + k], tile=t + 1)
        return up, dn

    for k in range(1, M):
        a2a(k).start()
    start_pair(fwd(0))
    loads[1].wait()
    loads[2].wait()
    kp = pair(kap_ref, halo_k, h_s, h_r, 0)
    rp = pair(r0_ref.at[m], halo_r, h_s, h_r, 2)
    start_pair(kp)
    start_pair(rp)
    gat[1, rows_of(m), :] = pf[m]

    @pl.when(jnp.logical_not(has_up))
    def _():
        gat[0] = jnp.zeros_like(gat[0])
        halo_k[0] = jnp.zeros_like(halo_k[0])
        halo_r[0] = jnp.zeros_like(halo_r[0])
        halo_q[0] = jnp.zeros_like(halo_q[0])

    @pl.when(jnp.logical_not(has_dn))
    def _():
        gat[2] = jnp.zeros_like(gat[2])
        halo_k[1] = jnp.zeros_like(halo_k[1])
        halo_r[1] = jnp.zeros_like(halo_r[1])
        halo_q[1] = jnp.zeros_like(halo_q[1])

    loads[3].wait()
    loads[4].wait()
    nobs = idx_ref.shape[1]
    step_obs = 256 if nobs % 256 == 0 else nobs
    weight = jnp.zeros((R, W), jnp.float32)
    for c in range(nobs // step_obs):
        idx = idx_ref[:, c * step_obs : (c + 1) * step_obs]
        prec = prec_ref[:, c * step_obs : (c + 1) * step_obs]
        line = idx // W - m * R
        col = idx % W
        hit = lax.broadcasted_iota(jnp.int32, (R, step_obs), 0) == line
        left = jnp.where(hit, prec, 0.0)
        first = left.astype(jnp.bfloat16)
        rest = left - first.astype(jnp.float32)
        second = rest.astype(jnp.bfloat16)
        third = (rest - second.astype(jnp.float32)).astype(jnp.bfloat16)
        hot = (lax.broadcasted_iota(jnp.int32, (W, step_obs), 0) == col)
        hot = jnp.where(hot, 1.0, 0.0).astype(jnp.bfloat16)
        for piece in (first, second, third):
            weight = weight + lax.dot_general(
                piece, hot, (((1,), (1,)), ((), ())), preferred_element_type=jnp.float32)

    for k in range(1, M):
        a2a_in(k).wait_recv()
        start_pair(fwd(k))

    recv_pair(kp)
    recv_pair(rp)
    kx = jnp.concatenate([halo_k[0], kap_ref[...], halo_k[1]], axis=0)
    lane = lax.broadcasted_iota(jnp.int32, (E, W), 1)
    line = lax.broadcasted_iota(jnp.int32, (E, W), 0)
    inside = (line + (t - 1) * R >= 0) & (line + (t - 1) * R < T * R)
    east = jnp.where(lane == W - 1, 0.0, pltpu.roll(kx, W - 1, axis=1))
    west = jnp.where(lane == 0, 0.0, pltpu.roll(kx, 1, axis=1))
    north = pltpu.roll(kx, 1, axis=0)
    south = pltpu.roll(kx, E - 1, axis=0)
    ce = 0.5 * (kx + east)
    cw = 0.5 * (kx + west)
    cn = 0.5 * (kx + north)
    cs = 0.5 * (kx + south)
    ca = 1.0 - ((ce + cw) + (cn + cs))
    ce = jnp.where(lane == W - 1, 0.0, ce)
    cw = jnp.where(lane == 0, 0.0, cw)
    for i, c in enumerate((ca, ce, cw, cn, cs)):
        c = jnp.where(inside, c, 0.0)
        for e in range(1, E - 1):
            cb[i, e] = jnp.broadcast_to(c[e : e + 1], (M, W))

    def turn(part):
        for j in range(W // 128):
            cols = slice(j * 128, (j + 1) * 128)
            block = gat[part, :, cols].reshape(M, R, 128)
            xt[part * R : (part + 1) * R, :, cols] = jnp.swapaxes(block, 0, 1)

    turn(1)
    for k in range(M):
        recv_pair(fwd(k))
    turn(0)
    turn(2)

    def localize():
        for e in range(E):
            xe = xt[e]
            fld[0, e] = xe * jnp.broadcast_to(ext[e : e + 1, :], (M, W))
        for s in range(SWEEPS):
            a, b = s % 2, (s + 1) % 2
            above, here = fld[a, s], fld[a, s + 1]
            for e in range(s + 1, E - 1 - s):
                below = fld[a, e + 1]
                out = cb[0, e] * here
                out = out + cb[3, e] * above
                out = out + cb[4, e] * below
                out = out + cb[1, e] * pltpu.roll(here, W - 1, axis=1)
                out = out + cb[2, e] * pltpu.roll(here, 1, axis=1)
                fld[b, e] = out
                above, here = here, below
        z = SWEEPS % 2
        for r in range(R):
            tot[r : r + 1, :] = jnp.sum(xt[R + r] * fld[z, R + r], axis=0, keepdims=True)
        return tot[...]

    def gather(buf, base):
        out = []
        for k in range(1, M):
            out.append(rc(buf.at[m], buf.at[m], g_s.at[base + k], g_r.at[base + k], mem=mem_at(k)))
        return out

    def gather_in(buf, base):
        for k in range(1, M):
            j = mem_from(k)
            rc(buf.at[j], buf.at[j], g_s.at[base + k], g_r.at[base + k], mem=mem_at(k)).wait_recv()

    me = t * M + m

    def all_at(k, sign):
        km, kt = k % M, k // M
        if sign > 0:
            return mem_at(km), lax.rem(t + kt, T)
        return mem_from(km), lax.rem(t + T - kt, T)

    def scal(n, k, slot):
        to_m, to_t = all_at(k, 1)
        at = n * M * T + k
        return rc(st.at[n, slot], st.at[n, slot], t_s.at[at], t_r.at[at], mem=to_m, tile=to_t)

    def sum_start(n, vals):
        lane1 = lax.broadcasted_iota(jnp.int32, (1, 128), 1)
        row = jnp.zeros((1, 128), jnp.float32)
        for i, v in enumerate(vals):
            row = jnp.where(lane1 == i, jnp.sum(v, axis=1, keepdims=True), row)
        st[n, me] = row
        for k in range(M * T - 1, 0, -1):
            c = scal(n, k, me)
            c.start()
            sends.append(c)

    def sum_end(n):
        for k in range(1, M * T):
            j_m, j_t = all_at(k, -1)
            scal(n, k, j_t * M + j_m).wait_recv()
        parts = [st[n, j] for j in range(M * T)]
        while len(parts) > 1:
            parts = [parts[i] + parts[i + 1] for i in range(0, len(parts) - 1, 2)] + (
                [parts[-1]] if len(parts) % 2 else [])
        return parts[0]

    inv = 1.0 / M
    r0 = r0_ref[m]
    ext[0:R] = halo_r[0]
    ext[R : 2 * R] = r0
    ext[2 * R : E] = halo_r[1]
    q0 = r0 + weight * r0 + localize() * inv
    q0a[m] = q0
    qp = pair(q0a.at[m], halo_q, q_s, q_r, 0)
    pl.semaphore_wait(go, T - 1)
    sum_start(0, (lanes_sum(r0 * r0), lanes_sum(r0 * q0)))
    start_pair(qp)
    g0 = gather(q0a, 0)
    for c in g0:
        c.start()
    recv_pair(qp)
    ext[0:R] = halo_q[0]
    ext[R : 2 * R] = q0
    ext[2 * R : E] = halo_q[1]
    q1 = q0 + weight * q0 + localize() * inv
    q1a[m] = q1
    g1 = gather(q1a, M)
    for c in g1:
        c.start()
    dots = sum_end(0)
    rr, rq = dots[:, 0:1], dots[:, 1:2]
    alpha = rr / rq
    r1 = r0 - alpha * q0
    ar1 = q0 - alpha * q1
    sum_start(1, (lanes_sum(r1 * r1), lanes_sum(r1 * ar1), lanes_sum(r1 * q0)))
    gather_in(q0a, 0)
    gather_in(q1a, M)
    dots = sum_end(1)
    new = dots[:, 0:1]
    beta = new / rr
    den = dots[:, 1:2] + 2.0 * beta * dots[:, 2:3] + beta * beta * rq
    alpha2 = new / den
    for l in range(levels):
        b = r0_ref[l]
        q = q0a[l]
        r1 = b - alpha * q
        inc_ref[l] = alpha * b + alpha2 * (r1 + beta * b)
        res_ref[l] = r1 - alpha2 * ((q - alpha * q1a[l]) + beta * q)

    for k in range(1, M):
        a2a(k).wait_send()
    for k in range(M):
        send_pair(fwd(k))
    send_pair(kp)
    send_pair(rp)
    send_pair(qp)
    for c in g0 + g1 + sends:
        c.wait_send()


def fused(M, T, right_side, members, diffusivity, obs_index, obs_precision):
    levels, R, W = right_side.shape
    f32 = jnp.float32
    dma = pltpu.SemaphoreType.DMA
    vmem = pl.BlockSpec(memory_space=pltpu.VMEM)
    out = pltpu.VMEM(right_side.shape, f32)
    E = 3 * R
    operands = (right_side, members, diffusivity, obs_index.reshape(1, -1), obs_precision.reshape(1, -1))
    return pl.pallas_call(
        functools.partial(kernel, M, T),
        name="cg",
        out_shape=(out, out),
        in_specs=[pl.BlockSpec(memory_space=pltpu.HBM)] * 5,
        out_specs=(vmem, vmem),
        scratch_shapes=[
            pltpu.VMEM((levels, R, W), f32),
            pltpu.VMEM((levels, R, W), members.dtype),
            pltpu.VMEM((R, W), f32),
            pltpu.VMEM((1, obs_index.shape[0]), jnp.int32),
            pltpu.VMEM((1, obs_index.shape[0]), f32),
            dma((5,)),
            pltpu.VMEM((levels, R, W), f32),
            pltpu.VMEM((3, M * R, W), f32),
            pltpu.VMEM((2, R, W), f32),
            pltpu.VMEM((2, R, W), f32),
            pltpu.VMEM((2, R, W), f32),
            pltpu.VMEM((E, M, W), f32),
            pltpu.VMEM((5, E, M, W), f32),
            pltpu.VMEM((2, E, M, W), f32),
            pltpu.VMEM((R, W), f32),
            pltpu.VMEM((E, W), f32),
            pltpu.VMEM((levels, R, W), f32),
            pltpu.VMEM((levels, R, W), f32),
            pltpu.VMEM((2, M * T, 1, 128), f32),
            pltpu.SemaphoreType.REGULAR,
            dma((M,)), dma((M,)),
            dma((2 * M,)), dma((2 * M,)),
            dma((4,)), dma((4,)),
            dma((2,)), dma((2,)),
            dma((2 * M,)), dma((2 * M,)),
            dma((2 * M * T,)), dma((2 * M * T,)),
        ],
        compiler_params=pltpu.CompilerParams(
            collective_id=0, has_side_effects=True),
    )(*[pltpu.with_memory_space_constraint(x, pltpu.HBM) for x in operands])


def padded(shard, sides, width):
    for axis, dim in sides:
        size, length = (lax.axis_size(axis), shard.shape[dim])
        up = [(i, (i + 1) % size) for i in range(size - 1)]
        down = [(j, i) for i, j in up]
        last = lax.slice_in_dim(shard, length - width, length, axis=dim)
        leading = lax.slice_in_dim(shard, 0, width, axis=dim)
        before = lax.ppermute(last, axis, up)
        after = lax.ppermute(leading, axis, down)
        shard = jnp.concatenate([before, shard, after], axis=dim)
    return shard


def sweep(field, kappa):
    centre = field[:, 1:-1]
    middle = kappa[:, 1:-1]
    flux = 0.5 * (middle + kappa[:, 2:]) * (field[:, 2:] - centre)
    flux = flux + 0.5 * (middle + kappa[:, :-2]) * (field[:, :-2] - centre)
    fpad = jnp.pad(centre, ((0, 0), (0, 0), (1, 1)))
    kpad = jnp.pad(middle, ((0, 0), (0, 0), (1, 1)))
    flux = flux + 0.5 * (middle + kpad[:, :, 2:]) * (fpad[:, :, 2:] - centre)
    flux = flux + 0.5 * (middle + kpad[:, :, :-2]) * (fpad[:, :, :-2] - centre)
    return centre + flux


def general(right_side, members, diffusivity, obs_index, obs_precision):
    levels, rows, width = right_side.shape
    level = obs_index // (rows * width)
    row_pos = obs_index // width % rows
    column = obs_index % width
    weight = jnp.zeros(right_side.shape, jnp.float32).at[level, row_pos, column].add(obs_precision)
    tile_pos = lax.axis_index("tile")
    all_rows = rows * lax.axis_size("tile")
    total_members = members.shape[0] * lax.axis_size("mem")
    depth_rim = SWEEPS
    kappa_rim = padded(diffusivity, (("tile", 1),), depth_rim)

    def inner(first, second):
        return lax.psum(jnp.sum(first * second), "tile")

    increment = jnp.zeros_like(right_side)
    residual, direction = (right_side, right_side)
    norm_now = inner(residual, residual)
    for step in range(ITERS):
        pert = members[0].astype(jnp.float32)
        extended = padded(pert * direction, (("tile", 1),), SWEEPS)
        for localize_step in range(SWEEPS):
            depth = SWEEPS - localize_step - 1
            kappa = kappa_rim[:, localize_step : kappa_rim.shape[1] - localize_step]
            extended = sweep(extended, kappa)
            global_row = tile_pos * rows - depth + jnp.arange(rows + 2 * depth, dtype=jnp.int32)
            inside = (global_row >= 0) & (global_row < all_rows)
            extended = jnp.where(inside[None, :, None], extended, 0.0)
        total = pert * extended
        operate_total = lax.psum(total, "mem")
        image = direction + weight * direction + operate_total / total_members
        alpha = norm_now / inner(direction, image)
        increment = increment + alpha * direction
        residual = residual - alpha * image
        if step + 1 < ITERS:
            norm_next = inner(residual, residual)
            direction = residual + norm_next / norm_now * direction
            norm_now = norm_next
    return (increment, residual)


def solution(mesh):
    in_specs = (
        P(None, "tile", None),
        P("mem", None, "tile", None),
        P(None, "tile", None),
        P("tile"),
        P("tile"),
    )
    out_specs = (P(None, "tile", None), P(None, "tile", None))
    M, T = mesh.shape["mem"], mesh.shape["tile"]

    def local(right_side, members, diffusivity, obs_index, obs_precision):
        levels, rows, width = right_side.shape
        fits = levels == M and members.shape[0] == 1 and rows == SWEEPS and M == 8
        if fits and ITERS == 2 and width % 128 == 0:
            return fused(M, T, right_side, members, diffusivity, obs_index, obs_precision)
        return general(right_side, members, diffusivity, obs_index, obs_precision)

    return jax.shard_map(local, mesh=mesh, in_specs=in_specs, out_specs=out_specs, check_vma=False)
```
